32 devices in a mesh: row: 4 (over z), leaf: 8 (over y, x, core).
Axes of the slice: x: 2, y: 2, z: 4, core: 2. Of those that a mesh axis runs over, the one named last changes fastest.
Arguments:
- leaf_update: float32 [16384, 256], P(('leaf', 'row')), may hold values from -6 to 6
- rhs: float32 [3, 16384, 256], P(None, ('leaf', 'row')), may hold values from -6 to 6
- inv_top: bfloat16 [2, 16384, 8, 4, 512], P(None, 'leaf', None, 'row'), may hold values from -0.03125 to 0.03125
- inv_mid: bfloat16 [2, 16384, 4, 4, 512], P(None, 'leaf', None, 'row'), may hold values from -0.046875 to 0.046875
- inv_low: bfloat16 [2, 16384, 2, 4, 512], P(None, 'leaf', None, 'row'), may hold values from -0.0625 to 0.0625
- couple_mid: bfloat16 [2, 16384, 4, 4, 512], P(None, 'leaf', None, 'row'), may hold values from -0.046875 to 0.046875
- couple_low: bfloat16 [2, 16384, 2, 4, 512], P(None, 'leaf', None, 'row'), may hold values from -0.0625 to 0.0625
- block_map: int32 [3, 128], P(None, ('leaf', 'row')), may hold values from 0 to 127, as said below
Outputs:
- solution: float32 [3, 16384, 256], P(None, ('leaf', 'row'))
- leaf_solution: float32 [16384, 256], P(('leaf', 'row'))
The draws below stay inside these ranges and needn't reach their ends.
Inputs may be any that keep to these rules, and one draw needn't show every extreme that they name: Device d of the group of a front holds rows d * 512 to (d + 1) * 512 - 1 of the front's separator part and the same rows of its update part, with d = p * 4 + r for group position p (leaf index modulo the group size) and row index r. block_map[k] is one to one within each parent, and a block held at row index r and group position p of a child lands on a parent block held at row index r and group position p or p + (group size of the parent) / 2. At level 0 every parent block receives one block.
All inputs are finite; a program needn't handle non-finite values.
Results may differ from the reference program's by a relative error of at most 0.012.
Values may be sent and summed in bfloat16 or wider, within the bound.
A program may use at most 256 MiB of HBM per device.

```python
import jax
import jax.numpy as jnp
from jax import lax

S_TOP = 16384
RHS = 128
BLOCK = 128
SLICE_ROWS = 512
BLOCKS_DEV = 4
SEP_MID = 8192
SEP_LOW = 4096
N_ROW = 4
N_LEAF = 8


def draw_block_map(key, part):
    levels = []
    for level_index in range(3):
        fronts = 2 ** level_index
        group_size = N_LEAF // fronts
        half_group = group_size // 2
        blocks_dev = BLOCKS_DEV
        per_side = blocks_dev * (2 if level_index > 0 else 1)
        pool_size = 2 * per_side
        sep_blocks = group_size * N_ROW * blocks_dev
        scores = jax.random.randint(jax.random.fold_in(key, 17 + level_index), (fronts, half_group, N_ROW, pool_size), 0, 1 << 20)
        scores = scores * pool_size + jnp.arange(pool_size, dtype=jnp.int32)
        picked = jnp.argsort(scores, axis=-1)[..., :2 * blocks_dev]
        side_index = picked // per_side
        remainder = picked % per_side
        kind_index = remainder // blocks_dev
        slot_index = remainder % blocks_dev
        position = jnp.arange(half_group, dtype=jnp.int32)[None, :, None, None]
        row_index = jnp.arange(N_ROW, dtype=jnp.int32)[None, None, :, None]
        holder = (side_index * half_group + position) * N_ROW + row_index
        targets = kind_index * sep_blocks + holder * blocks_dev + slot_index
        targets = targets.reshape(fronts, half_group, N_ROW, 2, blocks_dev).transpose(0, 3, 1, 2, 4)
        levels.append(targets.reshape(-1))
    return jnp.stack(levels).astype(jnp.int32)


def level_of(key, extent, split, low, high):
    def one(dim, blocks):
        draws = jax.random.uniform(jax.random.fold_in(jax.random.fold_in(key, 6), dim), (blocks,), jnp.float32, low / len(split), high / len(split))
        return jnp.repeat(jnp.exp(draws), extent[dim] // blocks).reshape((-1,) + (1,) * (len(extent) - dim - 1))

    level = one(*split[0])
    for cut in split[1:]:
        level = level * one(*cut)
    return level


def scatter_about(rng, dims, width, bound, pieces=(), held_as=jnp.bfloat16):
    array = jax.random.normal(rng, dims, jnp.float32) * width
    if len(pieces) > 0:
        array = level_of(rng, dims, pieces, -0.22, 0.18) * array
    return jnp.clip(array, min=-bound, max=bound).astype(held_as)


def setup_inputs(seed: int = 0) -> dict:
    key_list = jax.random.split(jax.random.key(seed), 9)
    return {
        "leaf_update": scatter_about(key_list[0], (S_TOP, 2 * RHS), 1.0, 6.0, ((0, 32),), jnp.float32),
        "rhs": scatter_about(key_list[1], (3, S_TOP, 2 * RHS), 1.0, 6.0, ((1, 32),), jnp.float32),
        "inv_top": scatter_about(key_list[2], (2, S_TOP, N_LEAF, N_ROW, SLICE_ROWS), (2 * S_TOP) ** -0.5, 0.03125, ((1, 8), (3, 4))),
        "inv_mid": scatter_about(key_list[3], (2, S_TOP, N_LEAF // 2, N_ROW, SLICE_ROWS), (2 * SEP_MID) ** -0.5, 0.046875, ((1, 8), (3, 4))),
        "inv_low": scatter_about(key_list[4], (2, S_TOP, N_LEAF // 4, N_ROW, SLICE_ROWS), (2 * SEP_LOW) ** -0.5, 0.0625, ((1, 8), (3, 4))),
        "couple_mid": scatter_about(key_list[5], (2, S_TOP, N_LEAF // 2, N_ROW, SLICE_ROWS), (2 * SEP_MID) ** -0.5, 0.046875, ((1, 8), (3, 4))),
        "couple_low": scatter_about(key_list[6], (2, S_TOP, N_LEAF // 4, N_ROW, SLICE_ROWS), (2 * SEP_LOW) ** -0.5, 0.0625, ((1, 8), (3, 4))),
        "block_map": draw_block_map(jax.random.fold_in(key_list[8], 71), 0),
    }


def complex_apply(real_part, imag_part, vector, transpose):
    half_cols = vector.shape[1] // 2
    right_side = vector.astype(jnp.bfloat16)
    if transpose:
        dim_numbers = (((0,), (0,)), ((), ()))
    else:
        dim_numbers = (((1,), (0,)), ((), ()))
    product_real = lax.dot_general(real_part, right_side, dim_numbers, preferred_element_type=jnp.float32)
    product_imag = lax.dot_general(imag_part, right_side, dim_numbers, preferred_element_type=jnp.float32)
    return jnp.concatenate([product_real[:, :half_cols] - product_imag[:, half_cols:], product_real[:, half_cols:] + product_imag[:, :half_cols]], axis=1)


def parent_index(targets, level_index, front_blocks):
    fronts = 2 ** level_index
    per_child = targets.shape[0] // (2 * fronts)
    parent_of = (jnp.arange(targets.shape[0], dtype=jnp.int32) // per_child) // 2
    return parent_of * front_blocks + targets


def reference(leaf_update, rhs, inv_top, inv_mid, inv_low, couple_mid, couple_low, block_map):
    columns = rhs.shape[2]
    inverses = [inv_top, inv_mid, inv_low]
    couplings = [None, couple_mid, couple_low]
    children = leaf_update
    saved_y = [None, None, None]
    for level_index in [2, 1, 0]:
        fronts = 2 ** level_index
        sep_rows = S_TOP // fronts
        has_update = level_index > 0
        front_blocks = (2 if has_update else 1) * (sep_rows // BLOCK)
        child_blocks = children.reshape(-1, BLOCK, columns)
        placed = parent_index(block_map[level_index], level_index, front_blocks)
        front_vec = jnp.zeros((fronts * front_blocks, BLOCK, columns), jnp.float32).at[placed].add(child_blocks)
        front_vec = front_vec.reshape(fronts, front_blocks * BLOCK, columns)
        sep_part = front_vec[:, :sep_rows] + rhs[level_index].reshape(fronts, sep_rows, columns)
        inverse = inverses[level_index].reshape(2, fronts, sep_rows, sep_rows)
        outputs_y = []
        updates = []
        for front_idx in range(fronts):
            solved = complex_apply(inverse[0, front_idx], inverse[1, front_idx], sep_part[front_idx], False)
            outputs_y.append(solved)
            if has_update:
                coupling = couplings[level_index].reshape(2, fronts, sep_rows, sep_rows)
                updates.append(front_vec[front_idx, sep_rows:] - complex_apply(coupling[0, front_idx], coupling[1, front_idx], solved, False))
        saved_y[level_index] = outputs_y
        if has_update:
            children = jnp.concatenate(updates, axis=0)
    solutions = []
    parent_flat = None
    for level_index in [0, 1, 2]:
        fronts = 2 ** level_index
        sep_rows = S_TOP // fronts
        inverse = inverses[level_index].reshape(2, fronts, sep_rows, sep_rows)
        if level_index > 0:
            parent_blocks = parent_flat.shape[0] // (2 ** (level_index - 1))
            taken_rows = parent_flat[parent_index(block_map[level_index - 1], level_index - 1, parent_blocks)]
            x_update = taken_rows.reshape(fronts, sep_rows, columns)
            coupling = couplings[level_index].reshape(2, fronts, sep_rows, sep_rows)
        level_x = []
        front_vectors = []
        for front_idx in range(fronts):
            reduced = saved_y[level_index][front_idx]
            if level_index > 0:
                reduced = reduced - complex_apply(coupling[0, front_idx], coupling[1, front_idx], x_update[front_idx], True)
            solved = complex_apply(inverse[0, front_idx], inverse[1, front_idx], reduced, True)
            level_x.append(solved)
            if level_index > 0:
                front_vectors.append(jnp.concatenate([solved, x_update[front_idx]], axis=0))
            else:
                front_vectors.append(solved)
        solutions.append(jnp.concatenate(level_x, axis=0))
        parent_flat = jnp.concatenate(front_vectors, axis=0).reshape(-1, BLOCK, columns)
    leaf_blocks = parent_flat[parent_index(block_map[2], 2, parent_flat.shape[0] // 4)]
    return jnp.stack(solutions), leaf_blocks.reshape(S_TOP, columns)
```

```python
import jax
import jax.numpy as jnp
from jax import lax
from jax.sharding import PartitionSpec as P

BLOCK = 128


def partner_2(block, axis, distance):
    count = lax.axis_size(axis)
    route = []
    for low in range(count):
        high = low | 1 << distance
        if high != low and high < count:
            route += [(low, high), (high, low)]
    return lax.ppermute(block, axis, route)


def turned(vector):
    half_cols = vector.shape[1] // 2
    return jnp.stack(
        [
            vector,
            jnp.concatenate([-vector[:, half_cols:], vector[:, :half_cols]], axis=1),
        ]
    )


def forward_apply(panel_tile, vector):
    positions, width = panel_tile.shape[2], panel_tile.shape[4]
    return lax.dot_general(
        panel_tile[:, :, :, 0, :],
        turned(vector).reshape(2, positions, width, -1),
        (((0, 2, 3), (0, 1, 2)), ((), ())),
        preferred_element_type=jnp.float32,
    )


def transposed_apply(panel_tile, vector):
    product = lax.dot_general(
        panel_tile[:, :, :, 0, :],
        turned(vector),
        (((0, 1), (0, 1)), ((), ())),
        preferred_element_type=jnp.float32,
    )
    return product.reshape(-1, vector.shape[1])


def subgroup_gather(vector, bit_count, leaf_pos):
    gathered = vector
    for bit_pos in range(bit_count):
        partner = partner_2(gathered, "leaf", bit_pos)
        upper_half = leaf_pos >> bit_pos & 1 == 1
        gathered = jnp.where(
            upper_half,
            jnp.concatenate([partner, gathered], axis=0),
            jnp.concatenate([gathered, partner], axis=0),
        )
    return gathered


def subgroup_sum(partial_value, bit_count, leaf_pos, order):
    rows = partial_value.shape[0] >> bit_count
    columns = partial_value.shape[1]
    shape = (2,) * bit_count + (rows, columns)
    total = partial_value.reshape(shape)
    left = list(range(bit_count))
    for bit_pos in order:
        axis = left[::-1].index(bit_pos)
        mine = leaf_pos >> bit_pos & 1
        keep = lax.dynamic_index_in_dim(total, mine, axis, keepdims=False)
        give = lax.dynamic_index_in_dim(total, 1 - mine, axis, keepdims=False)
        got = partner_2(give.astype(jnp.bfloat16), "leaf", bit_pos)
        total = keep + got.astype(jnp.float32)
        left.remove(bit_pos)
    return total.reshape(rows, columns)


def row_reduced(panel_tile, gathered):
    partial_value = forward_apply(panel_tile, gathered).astype(jnp.bfloat16)
    return lax.psum_scatter(partial_value, "row", scatter_dimension=0, tiled=True).astype(
        jnp.float32
    )


def row_folded(panel_tile, vector_half):
    return transposed_apply(panel_tile, lax.all_gather(vector_half, "row", axis=0, tiled=True))


def slot_ids(position, row_pos, row_size, blocks_dev, sep_blocks, has_update):
    own_slots = (position * row_size + row_pos) * blocks_dev + jnp.arange(
        blocks_dev, dtype=jnp.int32
    )
    if has_update:
        return jnp.concatenate([own_slots, own_slots + sep_blocks])
    return own_slots


def extend_add(child_rows, targets, rhs_part, bit_count, has_update, leaf_pos, row_pos, row_size):
    bit_pos = bit_count - 1
    partner_rows, partner_targets = partner_2((child_rows, targets), "leaf", bit_pos)
    blocks_dev = targets.shape[0]
    group_size = 1 << bit_count
    position = leaf_pos & group_size - 1
    sep_blocks = group_size * row_size * blocks_dev
    slot_list = slot_ids(position, row_pos, row_size, blocks_dev, sep_blocks, has_update)
    candidates = jnp.concatenate([targets, partner_targets])
    columns = child_rows.shape[1]
    block_pool = jnp.concatenate([child_rows, partner_rows], axis=0).reshape(2 * blocks_dev, -1)
    selector = (slot_list[:, None] == candidates[None, :]).astype(jnp.float32)
    placed = jnp.dot(
        selector, block_pool, precision=lax.Precision.HIGHEST, preferred_element_type=jnp.float32
    ).reshape(-1, columns)
    slice_rows = rhs_part.shape[0]
    return (placed[:slice_rows] + rhs_part, placed[slice_rows:])


def extend_down(front_rows, targets, bit_count, leaf_pos, row_pos, row_size):
    bit_pos = bit_count - 1
    partner_rows = partner_2(front_rows, "leaf", bit_pos)
    blocks_dev = targets.shape[0]
    has_update = front_rows.shape[0] > blocks_dev * BLOCK
    group_size = 1 << bit_count
    position = leaf_pos & group_size - 1
    sep_blocks = group_size * row_size * blocks_dev
    own_slots = slot_ids(position, row_pos, row_size, blocks_dev, sep_blocks, has_update)
    partner_slots = slot_ids(
        position ^ group_size // 2, row_pos, row_size, blocks_dev, sep_blocks, has_update
    )
    columns = front_rows.shape[1]
    block_pool = jnp.concatenate([front_rows, partner_rows], axis=0).reshape(-1, BLOCK * columns)
    selector = (targets[:, None] == jnp.concatenate([own_slots, partner_slots])[None, :]).astype(
        jnp.float32
    )
    return jnp.dot(
        selector, block_pool, precision=lax.Precision.HIGHEST, preferred_element_type=jnp.float32
    ).reshape(-1, columns)


def shards(leaf_update, rhs, inv_top, inv_mid, inv_low, couple_mid, couple_low, block_map):
    leaf_pos = lax.axis_index("leaf")
    row_pos = lax.axis_index("row")
    row_size = lax.axis_size("row")
    leaf_bits = lax.axis_size("leaf").bit_length() - 1
    inverses = (inv_top, inv_mid, inv_low)
    couplings = (None, couple_mid, couple_low)
    children = leaf_update
    saved_y = [None, None, None]
    for level_index in (2, 1):
        bit_count = leaf_bits - level_index
        sep_part, update_part = extend_add(
            children,
            block_map[level_index],
            rhs[level_index],
            bit_count,
            True,
            leaf_pos,
            row_pos,
            row_size,
        )
        gathered = subgroup_gather(sep_part.astype(jnp.bfloat16), bit_count, leaf_pos)
        solved = row_reduced(inverses[level_index], gathered)
        saved_y[level_index] = solved
        gathered_y = subgroup_gather(solved.astype(jnp.bfloat16), bit_count, leaf_pos)
        children = update_part - row_reduced(couplings[level_index], gathered_y)
    sep_top, unused_rows = extend_add(
        children, block_map[0], rhs[0], leaf_bits, False, leaf_pos, row_pos, row_size
    )
    gathered = lax.all_gather(sep_top.astype(jnp.bfloat16), "leaf", axis=0, tiled=True)
    y_top = row_reduced(inv_top, gathered)
    partial_value = row_folded(inv_top, y_top.astype(jnp.bfloat16))
    x_top = subgroup_sum(partial_value, leaf_bits, leaf_pos, range(leaf_bits))
    solutions = [x_top]
    front_rows = x_top
    for level_index in (1, 2):
        bit_count = leaf_bits - level_index
        x_update = extend_down(
            front_rows, block_map[level_index - 1], bit_count + 1, leaf_pos, row_pos, row_size
        )
        coupled = subgroup_sum(
            row_folded(couplings[level_index], x_update.astype(jnp.bfloat16)),
            bit_count,
            leaf_pos,
            range(bit_count),
        )
        reduced = saved_y[level_index] - coupled
        x_sep = subgroup_sum(
            row_folded(inverses[level_index], reduced.astype(jnp.bfloat16)),
            bit_count,
            leaf_pos,
            range(bit_count),
        )
        solutions.append(x_sep)
        front_rows = jnp.concatenate([x_sep, x_update], axis=0)
    leaf_solution = extend_down(
        front_rows, block_map[2], leaf_bits - 2, leaf_pos, row_pos, row_size
    )
    return (jnp.stack(solutions), leaf_solution)


def solution(mesh):
    return jax.shard_map(
        shards,
        mesh=mesh,
        in_specs=(
            P(("leaf", "row"), None),
            P(None, ("leaf", "row"), None),
            P(None, "leaf", None, "row", None),
            P(None, "leaf", None, "row", None),
            P(None, "leaf", None, "row", None),
            P(None, "leaf", None, "row", None),
            P(None, "leaf", None, "row", None),
            P(None, ("leaf", "row")),
        ),
        out_specs=(P(None, ("leaf", "row"), None), P(("leaf", "row"), None)),
        check_vma=False,
    )
```

```python
import jax
import jax.numpy as jnp
from jax import lax
from jax.sharding import PartitionSpec as P

BLOCK = 128


def partner_2(block, axis, distance):
    count = lax.axis_size(axis)
    route = []
    for low in range(count):
        high = low | 1 << distance
        if high != low and high < count:
            route += [(low, high), (high, low)]
    return lax.ppermute(block, axis, route)


def turned(vector):
    half_cols = vector.shape[1] // 2
    return jnp.stack(
        [
            vector,
            jnp.concatenate([-vector[:, half_cols:], vector[:, :half_cols]], axis=1),
        ]
    )


def forward_apply(panel_tile, vector):
    positions, width = panel_tile.shape[2], panel_tile.shape[4]
    return lax.dot_general(
        panel_tile[:, :, :, 0, :],
        turned(vector).reshape(2, positions, width, -1),
        (((0, 2, 3), (0, 1, 2)), ((), ())),
        preferred_element_type=jnp.float32,
    )


def transposed_apply(panel_tile, vector):
    product = lax.dot_general(
        panel_tile[:, :, :, 0, :],
        turned(vector),
        (((0, 1), (0, 1)), ((), ())),
        preferred_element_type=jnp.float32,
    )
    return product.reshape(-1, vector.shape[1])


def gather_in_order(vector, order, leaf_pos):
    bit_count = len(order)
    gathered = vector[None]
    done = []
    for bit_pos in order:
        partner = partner_2(gathered, "leaf", bit_pos)
        higher = [pos for pos in done if pos > bit_pos]
        done.append(bit_pos)
        outer = 1 << len(higher)
        mine = gathered.reshape(outer, 1, -1, *vector.shape)
        theirs = partner.reshape(mine.shape)
        upper_half = leaf_pos >> bit_pos & 1 == 1
        gathered = jnp.where(
            upper_half,
            jnp.concatenate([theirs, mine], axis=1),
            jnp.concatenate([mine, theirs], axis=1),
        ).reshape(-1, *vector.shape)
    return gathered.reshape((1 << bit_count) * vector.shape[0], vector.shape[1])


def subgroup_gather(vector, bit_count, leaf_pos):
    if bit_count < 3:
        return gather_in_order(vector, list(range(bit_count))[::-1], leaf_pos)
    outer_bits = list(range(1, bit_count))
    half_cols = vector.shape[1] // 2
    first = gather_in_order(vector[:, :half_cols], outer_bits + [0], leaf_pos)
    second = gather_in_order(vector[:, half_cols:], outer_bits[::-1] + [0], leaf_pos)
    return jnp.concatenate([first, second], axis=1)


def halved_sum(total, order, leaf_pos, left):
    for bit_pos in order:
        axis = left.index(bit_pos)
        mine = leaf_pos >> bit_pos & 1
        keep = lax.dynamic_index_in_dim(total, mine, axis, keepdims=False)
        give = lax.dynamic_index_in_dim(total, 1 - mine, axis, keepdims=False)
        got = partner_2(give.astype(jnp.bfloat16), "leaf", bit_pos)
        total = keep + got.astype(jnp.float32)
        left = [pos for pos in left if pos != bit_pos]
    return total


def subgroup_sum(partial_value, bit_count, leaf_pos):
    rows = partial_value.shape[0] >> bit_count
    columns = partial_value.shape[1]
    total = partial_value.reshape((2,) * bit_count + (rows, columns))
    left = list(range(bit_count))[::-1]
    if bit_count < 3:
        return halved_sum(total, left[::-1], leaf_pos, left)
    total = halved_sum(total, [0], leaf_pos, left)
    left = left[:-1]
    half_cols = columns // 2
    first = halved_sum(total[..., :half_cols], left, leaf_pos, left)
    second = halved_sum(total[..., half_cols:], left[::-1], leaf_pos, left)
    return jnp.concatenate([first, second], axis=1)


def row_reduced(panel_tile, gathered):
    partial_value = forward_apply(panel_tile, gathered).astype(jnp.bfloat16)
    return lax.psum_scatter(partial_value, "row", scatter_dimension=0, tiled=True).astype(
        jnp.float32
    )


def row_folded(panel_tile, vector_half):
    return transposed_apply(panel_tile, lax.all_gather(vector_half, "row", axis=0, tiled=True))


def slot_ids(position, row_pos, row_size, blocks_dev, sep_blocks, has_update):
    own_slots = (position * row_size + row_pos) * blocks_dev + jnp.arange(
        blocks_dev, dtype=jnp.int32
    )
    if has_update:
        return jnp.concatenate([own_slots, own_slots + sep_blocks])
    return own_slots


def extend_add(child_rows, targets, rhs_part, bit_count, has_update, leaf_pos, row_pos, row_size):
    bit_pos = bit_count - 1
    partner_targets = partner_2(targets, "leaf", bit_pos)
    partner_rows = partner_2(child_rows.astype(jnp.bfloat16), "leaf", bit_pos).astype(jnp.float32)
    blocks_dev = targets.shape[0]
    group_size = 1 << bit_count
    position = leaf_pos & group_size - 1
    sep_blocks = group_size * row_size * blocks_dev
    slot_list = slot_ids(position, row_pos, row_size, blocks_dev, sep_blocks, has_update)
    candidates = jnp.concatenate([targets, partner_targets])
    columns = child_rows.shape[1]
    block_pool = jnp.concatenate([child_rows, partner_rows], axis=0).reshape(2 * blocks_dev, -1)
    selector = (slot_list[:, None] == candidates[None, :]).astype(jnp.float32)
    placed = jnp.dot(
        selector, block_pool, precision=lax.Precision.HIGHEST, preferred_element_type=jnp.float32
    ).reshape(-1, columns)
    slice_rows = rhs_part.shape[0]
    return (placed[:slice_rows] + rhs_part, placed[slice_rows:])


def extend_down(front_rows, targets, bit_count, leaf_pos, row_pos, row_size):
    bit_pos = bit_count - 1
    partner_rows = partner_2(front_rows.astype(jnp.bfloat16), "leaf", bit_pos).astype(jnp.float32)
    blocks_dev = targets.shape[0]
    has_update = front_rows.shape[0] > blocks_dev * BLOCK
    group_size = 1 << bit_count
    position = leaf_pos & group_size - 1
    sep_blocks = group_size * row_size * blocks_dev
    own_slots = slot_ids(position, row_pos, row_size, blocks_dev, sep_blocks, has_update)
    partner_slots = slot_ids(
        position ^ group_size // 2, row_pos, row_size, blocks_dev, sep_blocks, has_update
    )
    columns = front_rows.shape[1]
    block_pool = jnp.concatenate([front_rows, partner_rows], axis=0).reshape(-1, BLOCK * columns)
    selector = (targets[:, None] == jnp.concatenate([own_slots, partner_slots])[None, :]).astype(
        jnp.float32
    )
    return jnp.dot(
        selector, block_pool, precision=lax.Precision.HIGHEST, preferred_element_type=jnp.float32
    ).reshape(-1, columns)


def shards(leaf_update, rhs, inv_top, inv_mid, inv_low, couple_mid, couple_low, block_map):
    leaf_pos = lax.axis_index("leaf")
    row_pos = lax.axis_index("row")
    row_size = lax.axis_size("row")
    leaf_bits = lax.axis_size("leaf").bit_length() - 1
    inverses = (inv_top, inv_mid, inv_low)
    couplings = (None, couple_mid, couple_low)
    children = leaf_update
    saved_y = [None, None, None]
    for level_index in (2, 1):
        bit_count = leaf_bits - level_index
        sep_part, update_part = extend_add(
            children,
            block_map[level_index],
            rhs[level_index],
            bit_count,
            True,
            leaf_pos,
            row_pos,
            row_size,
        )
        gathered = subgroup_gather(sep_part.astype(jnp.bfloat16), bit_count, leaf_pos)
        solved = row_reduced(inverses[level_index], gathered)
        saved_y[level_index] = solved
        gathered_y = subgroup_gather(solved.astype(jnp.bfloat16), bit_count, leaf_pos)
        children = update_part - row_reduced(couplings[level_index], gathered_y)
    sep_top, unused_rows = extend_add(
        children, block_map[0], rhs[0], leaf_bits, False, leaf_pos, row_pos, row_size
    )
    gathered = subgroup_gather(sep_top.astype(jnp.bfloat16), leaf_bits, leaf_pos)
    y_top = row_reduced(inv_top, gathered)
    partial_value = row_folded(inv_top, y_top.astype(jnp.bfloat16))
    x_top = subgroup_sum(partial_value, leaf_bits, leaf_pos)
    solutions = [x_top]
    front_rows = x_top
    for level_index in (1, 2):
        bit_count = leaf_bits - level_index
        x_update = extend_down(
            front_rows, block_map[level_index - 1], bit_count + 1, leaf_pos, row_pos, row_size
        )
        coupled = subgroup_sum(
            row_folded(couplings[level_index], x_update.astype(jnp.bfloat16)),
            bit_count,
            leaf_pos,
        )
        reduced = saved_y[level_index] - coupled
        x_sep = subgroup_sum(
            row_folded(inverses[level_index], reduced.astype(jnp.bfloat16)),
            bit_count,
            leaf_pos,
        )
        solutions.append(x_sep)
        front_rows = jnp.concatenate([x_sep, x_update], axis=0)
    leaf_solution = extend_down(
        front_rows, block_map[2], leaf_bits - 2, leaf_pos, row_pos, row_size
    )
    return (jnp.stack(solutions), leaf_solution)


def solution(mesh):
    return jax.shard_map(
        shards,
        mesh=mesh,
        in_specs=(
            P(("leaf", "row"), None),
            P(None, ("leaf", "row"), None),
            P(None, "leaf", None, "row", None),
            P(None, "leaf", None, "row", None),
            P(None, "leaf", None, "row", None),
            P(None, "leaf", None, "row", None),
            P(None, "leaf", None, "row", None),
            P(None, ("leaf", "row")),
        ),
        out_specs=(P(None, ("leaf", "row"), None), P(("leaf", "row"), None)),
        check_vma=False,
    )
```

```python
import jax
import jax.numpy as jnp
from jax import lax
from jax.sharding import PartitionSpec as P

BLOCK = 128


def partner_2(block, axis, distance):
    count = lax.axis_size(axis)
    route = []
    for low in range(count):
        high = low | 1 << distance
        if high != low and high < count:
            route += [(low, high), (high, low)]
    return lax.ppermute(block, axis, route)


def turned(vector):
    half_cols = vector.shape[1] // 2
    return jnp.stack(
        [
            vector,
            jnp.concatenate([-vector[:, half_cols:], vector[:, :half_cols]], axis=1),
        ]
    )


def forward_apply(panel_tile, vector):
    positions, width = panel_tile.shape[2], panel_tile.shape[4]
    return lax.dot_general(
        panel_tile[:, :, :, 0, :],
        turned(vector).reshape(2, positions, width, -1),
        (((0, 2, 3), (0, 1, 2)), ((), ())),
        preferred_element_type=jnp.float32,
    )


def transposed_apply(panel_tile, vector):
    product = lax.dot_general(
        panel_tile[:, :, :, 0, :],
        turned(vector),
        (((0, 1), (0, 1)), ((), ())),
        preferred_element_type=jnp.float32,
    )
    return product.reshape(-1, vector.shape[1])


def gather_in_order(vector, order, leaf_pos):
    bit_count = len(order)
    gathered = vector[None]
    done = []
    for bit_pos in order:
        partner = partner_2(gathered, "leaf", bit_pos)
        higher = [pos for pos in done if pos > bit_pos]
        done.append(bit_pos)
        outer = 1 << len(higher)
        mine = gathered.reshape(outer, 1, -1, *vector.shape)
        theirs = partner.reshape(mine.shape)
        upper_half = leaf_pos >> bit_pos & 1 == 1
        gathered = jnp.where(
            upper_half,
            jnp.concatenate([theirs, mine], axis=1),
            jnp.concatenate([mine, theirs], axis=1),
        ).reshape(-1, *vector.shape)
    return gathered.reshape((1 << bit_count) * vector.shape[0], vector.shape[1])


def subgroup_gather(vector, bit_count, leaf_pos):
    if bit_count < 3:
        return gather_in_order(vector, list(range(bit_count))[::-1], leaf_pos)
    outer_bits = list(range(1, bit_count))
    half_cols = vector.shape[1] // 2
    first = gather_in_order(vector[:, :half_cols], outer_bits + [0], leaf_pos)
    second = gather_in_order(vector[:, half_cols:], outer_bits[::-1] + [0], leaf_pos)
    return jnp.concatenate([first, second], axis=1)


def halved_sum(total, order, leaf_pos, left):
    for bit_pos in order:
        axis = left.index(bit_pos)
        mine = leaf_pos >> bit_pos & 1
        keep = lax.dynamic_index_in_dim(total, mine, axis, keepdims=False)
        give = lax.dynamic_index_in_dim(total, 1 - mine, axis, keepdims=False)
        got = partner_2(give.astype(jnp.bfloat16), "leaf", bit_pos)
        total = keep + got.astype(jnp.float32)
        left = [pos for pos in left if pos != bit_pos]
    return total


def subgroup_sum(partial_value, bit_count, leaf_pos):
    rows = partial_value.shape[0] >> bit_count
    columns = partial_value.shape[1]
    total = partial_value.reshape((2,) * bit_count + (rows, columns))
    left = list(range(bit_count))[::-1]
    if bit_count < 3:
        return halved_sum(total, left[::-1], leaf_pos, left)
    total = halved_sum(total, [0], leaf_pos, left)
    left = left[:-1]
    half_cols = columns // 2
    first = halved_sum(total[..., :half_cols], left, leaf_pos, left)
    second = halved_sum(total[..., half_cols:], left[::-1], leaf_pos, left)
    return jnp.concatenate([first, second], axis=1)


def row_reduced(panel_tile, gathered):
    partial_value = forward_apply(panel_tile, gathered).astype(jnp.bfloat16)
    return lax.psum_scatter(partial_value, "row", scatter_dimension=0, tiled=True).astype(
        jnp.float32
    )


def row_folded(panel_tile, vector_half):
    return transposed_apply(panel_tile, lax.all_gather(vector_half, "row", axis=0, tiled=True))


def slot_ids(position, row_pos, row_size, blocks_dev, sep_blocks, has_update):
    own_slots = (position * row_size + row_pos) * blocks_dev + jnp.arange(
        blocks_dev, dtype=jnp.int32
    )
    if has_update:
        return jnp.concatenate([own_slots, own_slots + sep_blocks])
    return own_slots


def extend_add(child_rows, targets, rhs_part, bit_count, has_update, leaf_pos, row_pos, row_size):
    bit_pos = bit_count - 1
    partner_targets = partner_2(targets, "leaf", bit_pos)
    partner_rows = partner_2(child_rows.astype(jnp.bfloat16), "leaf", bit_pos).astype(jnp.float32)
    blocks_dev = targets.shape[0]
    group_size = 1 << bit_count
    position = leaf_pos & group_size - 1
    sep_blocks = group_size * row_size * blocks_dev
    slot_list = slot_ids(position, row_pos, row_size, blocks_dev, sep_blocks, has_update)
    candidates = jnp.concatenate([targets, partner_targets])
    columns = child_rows.shape[1]
    block_pool = jnp.concatenate([child_rows, partner_rows], axis=0).reshape(2 * blocks_dev, -1)
    selector = (slot_list[:, None] == candidates[None, :]).astype(jnp.float32)
    placed = jnp.dot(
        selector, block_pool, precision=lax.Precision.HIGHEST, preferred_element_type=jnp.float32
    ).reshape(-1, columns)
    slice_rows = rhs_part.shape[0]
    return (placed[:slice_rows] + rhs_part, placed[slice_rows:])


def extend_down(front_parts, targets, bit_count, leaf_pos, row_pos, row_size):
    bit_pos = bit_count - 1
    partner_parts = [
        partner_2(part.astype(jnp.bfloat16), "leaf", bit_pos).astype(jnp.float32)
        for part in front_parts
    ]
    blocks_dev = targets.shape[0]
    has_update = len(front_parts) > 1
    group_size = 1 << bit_count
    position = leaf_pos & group_size - 1
    sep_blocks = group_size * row_size * blocks_dev
    own_slots = slot_ids(position, row_pos, row_size, blocks_dev, sep_blocks, has_update)
    partner_slots = slot_ids(
        position ^ group_size // 2, row_pos, row_size, blocks_dev, sep_blocks, has_update
    )
    columns = front_parts[0].shape[1]
    block_pool = jnp.concatenate([*front_parts, *partner_parts], axis=0).reshape(-1, BLOCK * columns)
    selector = (targets[:, None] == jnp.concatenate([own_slots, partner_slots])[None, :]).astype(
        jnp.float32
    )
    return jnp.dot(
        selector, block_pool, precision=lax.Precision.HIGHEST, preferred_element_type=jnp.float32
    ).reshape(-1, columns)


def shards(leaf_update, rhs, inv_top, inv_mid, inv_low, couple_mid, couple_low, block_map):
    leaf_pos = lax.axis_index("leaf")
    row_pos = lax.axis_index("row")
    row_size = lax.axis_size("row")
    leaf_bits = lax.axis_size("leaf").bit_length() - 1
    inverses = (inv_top, inv_mid, inv_low)
    couplings = (None, couple_mid, couple_low)
    children = leaf_update
    saved_y = [None, None, None]
    for level_index in (2, 1):
        bit_count = leaf_bits - level_index
        sep_part, update_part = extend_add(
            children,
            block_map[level_index],
            rhs[level_index],
            bit_count,
            True,
            leaf_pos,
            row_pos,
            row_size,
        )
        gathered = subgroup_gather(sep_part.astype(jnp.bfloat16), bit_count, leaf_pos)
        solved = row_reduced(inverses[level_index], gathered)
        saved_y[level_index] = solved
        gathered_y = subgroup_gather(solved.astype(jnp.bfloat16), bit_count, leaf_pos)
        children = update_part - row_reduced(couplings[level_index], gathered_y)
    sep_top, unused_rows = extend_add(
        children, block_map[0], rhs[0], leaf_bits, False, leaf_pos, row_pos, row_size
    )
    gathered = subgroup_gather(sep_top.astype(jnp.bfloat16), leaf_bits, leaf_pos)
    y_top = row_reduced(inv_top, gathered)
    partial_value = row_folded(inv_top, y_top.astype(jnp.bfloat16))
    x_top = subgroup_sum(partial_value, leaf_bits, leaf_pos)
    solutions = [x_top]
    front_parts = [x_top]
    for level_index in (1, 2):
        bit_count = leaf_bits - level_index
        x_update = extend_down(
            front_parts, block_map[level_index - 1], bit_count + 1, leaf_pos, row_pos, row_size
        )
        coupled = subgroup_sum(
            row_folded(couplings[level_index], x_update.astype(jnp.bfloat16)),
            bit_count,
            leaf_pos,
        )
        reduced = saved_y[level_index] - coupled
        x_sep = subgroup_sum(
            row_folded(inverses[level_index], reduced.astype(jnp.bfloat16)),
            bit_count,
            leaf_pos,
        )
        solutions.append(x_sep)
        front_parts = [x_sep, x_update]
    leaf_solution = extend_down(
        front_parts, block_map[2], leaf_bits - 2, leaf_pos, row_pos, row_size
    )
    return (jnp.stack(solutions), leaf_solution)


def solution(mesh):
    return jax.shard_map(
        shards,
        mesh=mesh,
        in_specs=(
            P(("leaf", "row"), None),
            P(None, ("leaf", "row"), None),
            P(None, "leaf", None, "row", None),
            P(None, "leaf", None, "row", None),
            P(None, "leaf", None, "row", None),
            P(None, "leaf", None, "row", None),
            P(None, "leaf", None, "row", None),
            P(None, ("leaf", "row")),
        ),
        out_specs=(P(None, ("leaf", "row"), None), P(("leaf", "row"), None)),
        check_vma=False,
    )
```
